1024 devices in a mesh: grp: 32 (over z, x_lo), dom: 32 (over x_hi, y, core).
Axes of the slice: x: 4 (x_hi: 2, x_lo: 2; x = x_hi * 2 + x_lo), y: 8, z: 16, core: 2. Of those that a mesh axis runs over, the one named last changes fastest.
Arguments:
- density: float32 [32, 256, 16384], P('grp', 'dom'), may hold values from -6 to 6
- diffusion: float32 [32, 256, 16384], P('grp', 'dom'), may hold values from 0.05 to 0.22
- drift_speed: float32 [32, 256, 16384], P('grp', 'dom'), may hold values from -0.3 to 0.3
- levels: int32 [32], P('grp'), may hold values from 5 to 8
- coefficient: int32 [32], P('grp'), may hold values from -2 to 2
Outputs:
- combined_field: float32 [32, 256, 16384], P('grp', 'dom')
The draws below stay inside these ranges and needn't reach their ends.
All inputs are finite; a program needn't handle non-finite values.
Results may differ from the reference program's by a relative error of at most 0.0003.
Values sent between devices are 32-bit elements; how exact they have to be, the bound alone decides.
A program may use at most 32 MiB of HBM per device.

```python
import math
import jax
import jax.numpy as jnp
import numpy as np
from jax import lax

S = 256
STEPS = 4
R = 16384
G = 32


def set_ends(entries, stream_key, least, top_value):
    index_at = [jax.random.randint(jax.random.fold_in(stream_key, axis), (), 0, length) for axis, length in enumerate(entries.shape)]
    longest = entries.shape.index(max(entries.shape))
    next_to = index_at[:longest] + [(index_at[longest] + 1) % entries.shape[longest]] + index_at[longest + 1:]
    return entries.at[tuple(index_at)].set(least).at[tuple(next_to)].set(top_value)


def shard_levels(rng, dims, split, low, top_value):
    def one(dim, blocks):
        heights = jax.random.uniform(jax.random.fold_in(jax.random.fold_in(rng, 6), dim), (blocks,), jnp.float32, low / len(split), top_value / len(split))
        return jnp.repeat(jnp.exp(heights), dims[dim] // blocks).reshape((-1,) + (1,) * (len(dims) - dim - 1))

    factor_of = one(*split[0])
    for cut in split[1:]:
        factor_of = factor_of * one(*cut)
    return factor_of


def gaussian(rng, dims, spread, bound, pieces=(), kind=jnp.bfloat16):
    gain = shard_levels(rng, dims, pieces, -0.22, 0.18) if pieces else 1.0
    entries = jax.random.normal(rng, dims, jnp.float32) * spread * gain
    return jnp.minimum(jnp.maximum(entries, -bound), bound).astype(kind)


def setup_inputs(seed: int = 0) -> dict:
    seeds = jax.random.split(jax.random.key(seed), 6)
    density = gaussian(seeds[0], (G, S, R), 1.0, 6.0, ((0, 32), (1, 32)), jnp.float32)
    diffusion = jnp.clip(jnp.exp(math.log(0.22) - 1.48160452 * jax.random.uniform(seeds[1], (G, S, R), jnp.float32) ** shard_levels(seeds[1], (G, S, R), ((0, 32), (1, 32)), -0.2, 0.2)), 0.05, 0.22)
    drift_speed = jnp.clip(jax.random.uniform(seeds[2], (G, S, R), jnp.float32, -0.3, 0.3) * shard_levels(seeds[2], (G, S, R), ((0, 32), (1, 32)), -0.4, 0.0), -0.3, 0.3)
    levels = set_ends(jax.random.randint(seeds[3], (G,), 5, 9), jax.random.fold_in(seeds[3], 1), 5, 8).astype(jnp.int32)
    coefficient = set_ends(jax.random.randint(seeds[4], (G,), -2, 3), jax.random.fold_in(seeds[4], 1), -2, 2).astype(jnp.int32)
    return {"density": density, "diffusion": diffusion, "drift_speed": drift_speed, "levels": levels, "coefficient": coefficient}


def hier_tables(size):
    to_surplus = np.zeros((size, size), dtype=np.float32)
    to_nodal = np.zeros((size, size), dtype=np.float32)
    node_level = np.zeros((size,), dtype=np.int32)
    depth = size.bit_length() - 1
    spots = np.arange(1, size + 1, dtype=np.float32)
    for index in range(size):
        position = index + 1
        to_surplus[index, index] = 1.0
        if position == size:
            node_level[index] = 0
            to_nodal[:, index] = spots / size
            continue
        stride = 1
        zeros_count = 0
        while position % (2 * stride) == 0:
            stride = stride * 2
            zeros_count = zeros_count + 1
        node_level[index] = depth - zeros_count
        to_nodal[:, index] = np.maximum(0.0, 1.0 - np.abs(spots - position) / stride)
        if position - stride > 0:
            to_surplus[index, position - stride - 1] -= 0.5
        if position + stride <= size:
            to_surplus[index, position + stride - 1] -= 0.5
    return to_surplus, to_nodal, node_level


def advance(state, diffuse, drifts):
    padded = jnp.pad(state, 1)
    above_cell = padded[2:, 1:-1]
    below_cell = padded[:-2, 1:-1]
    right_cell = padded[1:-1, 2:]
    left_cell = padded[1:-1, :-2]
    return state + diffuse * (above_cell + below_cell + right_cell + left_cell - 4.0 * state) - 0.5 * drifts * (above_cell - below_cell)


def reference(density, diffusion, drift_speed, levels, coefficient):
    to_surplus, to_nodal, node_level = hier_tables(S)
    to_surplus = jnp.asarray(to_surplus)
    to_nodal = jnp.asarray(to_nodal)
    node_level = jnp.asarray(node_level)

    def one_grid(items):
        state, diffuse, drifts, level_one, coef_one = items
        for sweep in range(STEPS):
            state = advance(state, diffuse, drifts)
        surplus = jnp.dot(to_surplus, state, precision=lax.Precision.HIGHEST, preferred_element_type=jnp.float32)
        member_mask = (node_level <= level_one).astype(jnp.float32)
        return surplus * (member_mask * coef_one.astype(jnp.float32))[:, None]

    weighted = lax.map(one_grid, (density, diffusion, drift_speed, levels, coefficient))
    total = jnp.sum(weighted, axis=0)

    def back_grid(level_one):
        member_mask = (node_level <= level_one).astype(jnp.float32)
        return jnp.dot(to_nodal, total * member_mask[:, None], precision=lax.Precision.HIGHEST, preferred_element_type=jnp.float32)

    return lax.map(back_grid, levels)
```

```python
import jax
import jax.numpy as jnp
from jax import lax
from jax.experimental import pallas as pl
from jax.experimental.pallas import tpu as pltpu
from jax.sharding import PartitionSpec as P

MESH = pl.DeviceIdType.MESH
CHUNKS = 4
Z = 16
DOM = 32
EDGES = ((0, 6), (6, 10), (10, 14), (14, 18))
FAR_FIRST = (8, 7, 9, 6, 10, 5, 11, 4, 12, 3, 13, 2, 14, 1, 15)


def kernel(
    lev_ref, coef_ref, den_ref, dif_ref, dri_ref, out_ref,
    in_d, in_k, in_v, D, K, V, A, B, W, RX, PZ, RZ, G, H,
    load_sem, halo_send, halo_recv, xs, xr, zs, zr, gs, gr, xgs, xgr, hs, hr,
):
    grp = lax.axis_index("grp")
    dom = lax.axis_index("dom")
    z = grp // 2
    x = grp % 2
    xo = 1 - x
    has_up = dom > 0
    has_down = dom < DOM - 1
    peer_x = (z * 2 + xo, dom)

    def z_peer(k):
        return (((z + k) % Z) * 2 + x, dom)

    loads = [
        pltpu.make_async_copy(src, dst, load_sem.at[i])
        for i, (src, dst) in enumerate(((den_ref, in_d), (dif_ref, in_k), (dri_ref, in_v)))
    ]
    for load in loads:
        load.start()

    barrier = pltpu.get_barrier_semaphore()

    def greet(device):
        pl.semaphore_signal(barrier, inc=1, device_id=device, device_id_type=MESH)

    for k in FAR_FIRST:
        greet(z_peer(k))
    greet(peer_x)

    @pl.when(has_up)
    def _():
        greet((grp, dom - 1))
        greet((z * 2 + xo, dom - 1))

    @pl.when(has_down)
    def _():
        greet((grp, dom + 1))
        greet((z * 2 + xo, dom + 1))

    sub = lax.broadcasted_iota(jnp.int32, (8, 128), 0)
    lane = lax.broadcasted_iota(jnp.int32, (8, 128), 1)
    zero = jnp.zeros((8, 128), jnp.float32)

    @pl.when(dom == 0)
    def _():
        D[0:5] = jnp.zeros((5, 18, 8, 128), jnp.float32)
        K[0:4] = jnp.zeros((4, 18, 8, 128), jnp.float32)
        V[0:4] = jnp.zeros((4, 18, 8, 128), jnp.float32)

    @pl.when(dom == DOM - 1)
    def _():
        D[13:17] = jnp.zeros((4, 18, 8, 128), jnp.float32)
        K[12:15] = jnp.zeros((3, 18, 8, 128), jnp.float32)
        V[12:15] = jnp.zeros((3, 18, 8, 128), jnp.float32)

    def halo(direction, array, c):
        lo, hi = EDGES[c]
        ref = (D, K, V)[array]
        if direction == 0:
            src, dst, n = (8, 0, 5) if array == 0 else (8, 0, 4)
            to = (grp, dom + 1)
        else:
            src, dst, n = (5, 13, 4) if array == 0 else (4, 12, 3)
            to = (grp, dom - 1)
        return pltpu.make_async_remote_copy(
            src_ref=ref.at[pl.ds(src, n), pl.ds(lo, hi - lo)],
            dst_ref=ref.at[pl.ds(dst, n), pl.ds(lo, hi - lo)],
            send_sem=halo_send.at[direction, array, c],
            recv_sem=halo_recv.at[direction, array, c],
            device_id=to,
            device_id_type=MESH,
        )

    def spread(c):
        for source, ref, first in ((in_d, D, 5), (in_k, K, 4), (in_v, V, 4)):
            for e in range(*EDGES[c]):
                for r in range(8):
                    a = (e - 1) % 16
                    tile = source[pl.ds(a * 8 + r, 8, stride=128), :]
                    if e == 0:
                        tile = jnp.where(sub == 0, zero, pltpu.roll(tile, 1, 0))
                    if e == 17:
                        tile = jnp.where(sub == 7, zero, pltpu.roll(tile, 7, 0))
                    ref[first + r, e] = tile

    for load in loads:
        load.wait()
    for c in range(CHUNKS):
        spread(c)
        if c == 0:
            pl.semaphore_wait(
                barrier,
                Z + 2 * has_up.astype(jnp.int32) + 2 * has_down.astype(jnp.int32),
            )

        @pl.when(has_down)
        def _():
            for array in range(3):
                halo(0, array, c).start()

        @pl.when(has_up)
        def _():
            for array in range(3):
                halo(1, array, c).start()

    level = lev_ref[0]
    coef = coef_ref[0].astype(jnp.float32)
    keep = [
        jnp.minimum(jnp.maximum(level - (finest - 1), 0), 1).astype(jnp.float32)
        for finest in (6, 7, 8)
    ]

    def step(src, dst, first, last, c, offset, inner):
        for r in range(first, last + 1):
            mid = [src[r + 5, offset + j] for j in range(6)]
            from_left = [pltpu.roll(t, 1, 1) for t in mid]
            from_right = [pltpu.roll(t, 127, 1) for t in mid]
            for j in inner:
                left = from_left[j]
                right = from_right[j]
                if j > 0:
                    left = jnp.where(lane == 0, from_left[j - 1], left)
                if j < 5:
                    right = jnp.where(lane == 127, from_right[j + 1], right)
                below = src[r + 4, offset + j]
                above = src[r + 6, offset + j]
                dst[r + 5, j] = (
                    mid[j]
                    + K[r + 4, 4 * c + j] * (above + below + right + left - 4.0 * mid[j])
                    - 0.5 * V[r + 4, 4 * c + j] * (above - below)
                )

    def x_send(c):
        return pltpu.make_async_remote_copy(
            src_ref=W.at[c, xo], dst_ref=RX.at[c],
            send_sem=xs.at[c], recv_sem=xr.at[c],
            device_id=peer_x, device_id_type=MESH,
        )

    def z_send(c, k):
        return pltpu.make_async_remote_copy(
            src_ref=PZ.at[c, (z + k) % Z], dst_ref=RZ.at[c, k - 1],
            send_sem=zs.at[c], recv_sem=zr.at[c],
            device_id=z_peer(k), device_id_type=MESH,
        )

    def g_send(c, k):
        return pltpu.make_async_remote_copy(
            src_ref=G.at[c, x, z], dst_ref=G.at[c, x, z],
            send_sem=gs.at[c], recv_sem=gr.at[c],
            device_id=z_peer(k), device_id_type=MESH,
        )

    def xg_send(c):
        return pltpu.make_async_remote_copy(
            src_ref=G.at[c, x], dst_ref=G.at[c, x],
            send_sem=xgs.at[c], recv_sem=xgr.at[c],
            device_id=peer_x, device_id_type=MESH,
        )

    def h_send(c, other):
        return pltpu.make_async_remote_copy(
            src_ref=G.at[c, x, pl.ds(14, 2)], dst_ref=H.at[c, x],
            send_sem=hs.at[c, other], recv_sem=hr.at[c, other],
            device_id=(z * 2 + (xo if other else x), dom + 1), device_id_type=MESH,
        )

    def all_bytes(c, sem):
        return pltpu.make_async_copy(RZ.at[c], RZ.at[c], sem.at[c])

    def advance(c):
        @pl.when(has_up)
        def _():
            for array in range(3):
                halo(0, array, c).wait_recv()

        @pl.when(has_down)
        def _():
            for array in range(3):
                halo(1, array, c).wait_recv()

        every = range(6)
        step(D, A, -4, 10, c, 4 * c, every)
        step(A, B, -3, 9, c, 0, every)
        step(B, A, -2, 8, c, 0, every)
        step(A, B, -1, 7, c, 0, range(1, 5))
        w6, w7, w8 = (coef * k for k in keep)
        for a in range(4):
            s = [B[r + 5, a + 1] for r in range(-1, 8)]
            prev, s = s[0], s[1:]
            weighted = [
                w8 * (s[0] - 0.5 * (prev + s[1])),
                w7 * (s[1] - 0.5 * (prev + s[3])),
                w8 * (s[2] - 0.5 * (s[1] + s[3])),
                w6 * (s[3] - 0.5 * (prev + s[7])),
                w8 * (s[4] - 0.5 * (s[3] + s[5])),
                w7 * (s[5] - 0.5 * (s[3] + s[7])),
                w8 * (s[6] - 0.5 * (s[5] + s[7])),
                coef * s[7],
            ]
            for r in range(8):
                W[c, a // 2, 2 * r + a % 2] = weighted[r]
        x_send(c).start()

    def pair_sum(c):
        x_send(c).wait_recv()
        for p in range(16):
            PZ[c, p] = W[c, x, p] + RX[c, p]
        for k in FAR_FIRST:
            z_send(c, k).start()

    def ring_sum(c):
        all_bytes(c, zr).wait()
        total = PZ[c, z]
        for k in range(15):
            total = total + RZ[c, k]
        G[c, x, z] = total
        for k in FAR_FIRST:
            g_send(c, k).start()

    def share(c):
        all_bytes(c, gr).wait()
        xg_send(c).start()

        @pl.when(has_down)
        def _():
            h_send(c, 0).start()
            h_send(c, 1).start()

    def nodal(c):
        xg_send(c).wait_recv()

        @pl.when(has_up)
        def _():
            h_send(c, 0).wait_recv()
            h_send(c, 1).wait_recv()

        m6, m7, m8 = keep
        for a in range(4):
            t = [G[c, a // 2, 2 * r + a % 2] for r in range(8)]
            prev = H[c, a // 2, a % 2]
            o7 = t[7]
            o3 = 0.5 * (prev + o7) + m6 * t[3]
            o1 = 0.5 * (prev + o3) + m7 * t[1]
            o5 = 0.5 * (o3 + o7) + m7 * t[5]
            o0 = 0.5 * (prev + o1) + m8 * t[0]
            o2 = 0.5 * (o1 + o3) + m8 * t[2]
            o4 = 0.5 * (o3 + o5) + m8 * t[4]
            o6 = 0.5 * (o5 + o7) + m8 * t[6]
            for r, o in enumerate((o0, o1, o2, o3, o4, o5, o6, o7)):
                out_ref[pl.ds((4 * c + a) * 8 + r, 8, stride=128), :] = o

    @pl.when(dom == 0)
    def _():
        H[...] = jnp.zeros((CHUNKS, 2, 2, 8, 128), jnp.float32)

    for stage, c in (
        (advance, 0), (advance, 1), (pair_sum, 0), (advance, 2), (pair_sum, 1), (advance, 3), (pair_sum, 2),
        (ring_sum, 0), (pair_sum, 3), (ring_sum, 1), (share, 0), (ring_sum, 2), (share, 1), (nodal, 0),
        (ring_sum, 3), (share, 2), (nodal, 1), (share, 3), (nodal, 2), (nodal, 3),
    ):
        stage(c)

    for c in range(CHUNKS):
        x_send(c).wait_send()
        all_bytes(c, zs).wait()
        all_bytes(c, gs).wait()
        xg_send(c).wait_send()

        @pl.when(has_down)
        def _():
            for array in range(3):
                halo(0, array, c).wait_send()
            h_send(c, 0).wait_send()
            h_send(c, 1).wait_send()

        @pl.when(has_up)
        def _():
            for array in range(3):
                halo(1, array, c).wait_send()


def on_device(density, diffusion, drift_speed, levels, coefficient):
    def tiles(block):
        return block.reshape(8, 128, 128).transpose(1, 0, 2).reshape(1024, 128)

    f32 = jnp.float32
    out = pl.pallas_call(
        kernel,
        out_shape=jax.ShapeDtypeStruct((1024, 128), f32),
        in_specs=[pl.BlockSpec(memory_space=pltpu.SMEM)] * 2 + [pl.BlockSpec(memory_space=pl.ANY)] * 3,
        out_specs=pl.BlockSpec(memory_space=pltpu.VMEM),
        scratch_shapes=[
            pltpu.VMEM((1024, 128), f32),
            pltpu.VMEM((1024, 128), f32),
            pltpu.VMEM((1024, 128), f32),
            pltpu.VMEM((17, 18, 8, 128), f32),
            pltpu.VMEM((15, 18, 8, 128), f32),
            pltpu.VMEM((15, 18, 8, 128), f32),
            pltpu.VMEM((17, 6, 8, 128), f32),
            pltpu.VMEM((17, 6, 8, 128), f32),
            pltpu.VMEM((CHUNKS, 2, 16, 8, 128), f32),
            pltpu.VMEM((CHUNKS, 16, 8, 128), f32),
            pltpu.VMEM((CHUNKS, 16, 8, 128), f32),
            pltpu.VMEM((CHUNKS, 15, 8, 128), f32),
            pltpu.VMEM((CHUNKS, 2, 16, 8, 128), f32),
            pltpu.VMEM((CHUNKS, 2, 2, 8, 128), f32),
            pltpu.SemaphoreType.DMA((3,)),
            pltpu.SemaphoreType.DMA((2, 3, CHUNKS)),
            pltpu.SemaphoreType.DMA((2, 3, CHUNKS)),
            pltpu.SemaphoreType.DMA((CHUNKS,)),
            pltpu.SemaphoreType.DMA((CHUNKS,)),
            pltpu.SemaphoreType.DMA((CHUNKS,)),
            pltpu.SemaphoreType.DMA((CHUNKS,)),
            pltpu.SemaphoreType.DMA((CHUNKS,)),
            pltpu.SemaphoreType.DMA((CHUNKS,)),
            pltpu.SemaphoreType.DMA((CHUNKS,)),
            pltpu.SemaphoreType.DMA((CHUNKS,)),
            pltpu.SemaphoreType.DMA((CHUNKS, 2)),
            pltpu.SemaphoreType.DMA((CHUNKS, 2)),
        ],
        compiler_params=pltpu.CompilerParams(collective_id=0, has_side_effects=True),
        name="combine",
    )(levels, coefficient, tiles(density[0]), tiles(diffusion[0]), tiles(drift_speed[0]))
    return out.reshape(128, 8, 128).transpose(1, 0, 2).reshape(1, 8, 16384)


def solution(mesh):
    return jax.shard_map(
        on_device,
        mesh=mesh,
        in_specs=(
            P("grp", "dom", None),
            P("grp", "dom", None),
            P("grp", "dom", None),
            P("grp"),
            P("grp"),
        ),
        out_specs=P("grp", "dom", None),
        check_vma=False,
    )
```

```python
import jax
import jax.numpy as jnp
from jax import lax
from jax.experimental import pallas as pl
from jax.experimental.pallas import tpu as pltpu
from jax.sharding import PartitionSpec as P

MESH = pl.DeviceIdType.MESH
CHUNKS = 4
Z = 16
DOM = 32
EDGES = ((0, 6), (6, 10), (10, 14), (14, 18))
FAR_FIRST = (8, 7, 9, 6, 10, 5, 11, 4, 12, 3, 13, 2, 14, 1, 15)


def kernel(
    lev_ref, coef_ref, den_ref, dif_ref, dri_ref, out_ref,
    in_d, in_k, in_v, D, K, V, A, B, W, RX, PZ, RZ, G, H,
    load_sem, halo_send, halo_recv, chain_sem, open_sem, xs, xr, zs, zr, gs, gr, xgs, xgr, hs, hr,
):
    grp = lax.axis_index("grp")
    dom = lax.axis_index("dom")
    z = grp // 2
    x = grp % 2
    xo = 1 - x
    has_up = dom > 0
    has_down = dom < DOM - 1
    peer_x = (z * 2 + xo, dom)

    def z_peer(k):
        return (((z + k + Z) % Z) * 2 + x, dom)

    loads = [
        pltpu.make_async_copy(src, dst, load_sem.at[i])
        for i, (src, dst) in enumerate(((den_ref, in_d), (dif_ref, in_k), (dri_ref, in_v)))
    ]
    for load in loads:
        load.start()

    barrier = pltpu.get_barrier_semaphore()

    def greet(device):
        pl.semaphore_signal(barrier, inc=1, device_id=device, device_id_type=MESH)

    greet(peer_x)

    @pl.when(z > 0)
    def _():
        greet(z_peer(-1))

    @pl.when(z < Z - 1)
    def _():
        greet(z_peer(1))

    @pl.when(has_up)
    def _():
        greet((grp, dom - 1))
        greet((z * 2 + xo, dom - 1))

    @pl.when(has_down)
    def _():
        greet((grp, dom + 1))
        greet((z * 2 + xo, dom + 1))

    sub = lax.broadcasted_iota(jnp.int32, (8, 128), 0)
    lane = lax.broadcasted_iota(jnp.int32, (8, 128), 1)
    zero = jnp.zeros((8, 128), jnp.float32)

    @pl.when(dom == 0)
    def _():
        D[0:5] = jnp.zeros((5, 18, 8, 128), jnp.float32)
        K[0:4] = jnp.zeros((4, 18, 8, 128), jnp.float32)
        V[0:4] = jnp.zeros((4, 18, 8, 128), jnp.float32)

    @pl.when(dom == DOM - 1)
    def _():
        D[13:17] = jnp.zeros((4, 18, 8, 128), jnp.float32)
        K[12:15] = jnp.zeros((3, 18, 8, 128), jnp.float32)
        V[12:15] = jnp.zeros((3, 18, 8, 128), jnp.float32)

    def halo(direction, array, c):
        lo, hi = EDGES[c]
        ref = (D, K, V)[array]
        if direction == 0:
            src, dst, n = (8, 0, 5) if array == 0 else (8, 0, 4)
            to = (grp, dom + 1)
        else:
            src, dst, n = (5, 13, 4) if array == 0 else (4, 12, 3)
            to = (grp, dom - 1)
        return pltpu.make_async_remote_copy(
            src_ref=ref.at[pl.ds(src, n), pl.ds(lo, hi - lo)],
            dst_ref=ref.at[pl.ds(dst, n), pl.ds(lo, hi - lo)],
            send_sem=halo_send.at[direction, array, c],
            recv_sem=halo_recv.at[direction, array, c],
            device_id=to,
            device_id_type=MESH,
        )

    def spread(c):
        for source, ref, first in ((in_d, D, 5), (in_k, K, 4), (in_v, V, 4)):
            for e in range(*EDGES[c]):
                for r in range(8):
                    a = (e - 1) % 16
                    tile = source[pl.ds(a * 8 + r, 8, stride=128), :]
                    if e == 0:
                        tile = jnp.where(sub == 0, zero, pltpu.roll(tile, 1, 0))
                    if e == 17:
                        tile = jnp.where(sub == 7, zero, pltpu.roll(tile, 7, 0))
                    ref[first + r, e] = tile

    for load in loads:
        load.wait()
    for c in range(CHUNKS):
        spread(c)
        if c == 0:
            pl.semaphore_wait(
                barrier,
                1 + (z > 0).astype(jnp.int32) + (z < Z - 1).astype(jnp.int32)
                + 2 * has_up.astype(jnp.int32) + 2 * has_down.astype(jnp.int32),
            )

        @pl.when(has_down)
        def _():
            for array in range(3):
                halo(0, array, c).start()

        @pl.when(has_up)
        def _():
            for array in range(3):
                halo(1, array, c).start()

    @pl.when(z > 0)
    def _():
        pl.semaphore_wait(chain_sem, 1)

    @pl.when(z < Z - 1)
    def _():
        pl.semaphore_signal(chain_sem, inc=1, device_id=z_peer(1), device_id_type=MESH)

    @pl.when(z == Z - 1)
    def _():
        for k in FAR_FIRST:
            pl.semaphore_signal(open_sem, inc=1, device_id=z_peer(k), device_id_type=MESH)

    level = lev_ref[0]
    coef = coef_ref[0].astype(jnp.float32)
    keep = [
        jnp.minimum(jnp.maximum(level - (finest - 1), 0), 1).astype(jnp.float32)
        for finest in (6, 7, 8)
    ]

    def step(src, dst, first, last, c, offset, inner):
        for r in range(first, last + 1):
            mid = [src[r + 5, offset + j] for j in range(6)]
            from_left = [pltpu.roll(t, 1, 1) for t in mid]
            from_right = [pltpu.roll(t, 127, 1) for t in mid]
            for j in inner:
                left = from_left[j]
                right = from_right[j]
                if j > 0:
                    left = jnp.where(lane == 0, from_left[j - 1], left)
                if j < 5:
                    right = jnp.where(lane == 127, from_right[j + 1], right)
                below = src[r + 4, offset + j]
                above = src[r + 6, offset + j]
                dst[r + 5, j] = (
                    mid[j]
                    + K[r + 4, 4 * c + j] * (above + below + right + left - 4.0 * mid[j])
                    - 0.5 * V[r + 4, 4 * c + j] * (above - below)
                )

    def x_send(c):
        return pltpu.make_async_remote_copy(
            src_ref=W.at[c, xo], dst_ref=RX.at[c],
            send_sem=xs.at[c], recv_sem=xr.at[c],
            device_id=peer_x, device_id_type=MESH,
        )

    def z_send(c, k):
        return pltpu.make_async_remote_copy(
            src_ref=PZ.at[c, (z + k) % Z], dst_ref=RZ.at[c, k - 1],
            send_sem=zs.at[c], recv_sem=zr.at[c],
            device_id=z_peer(k), device_id_type=MESH,
        )

    def g_send(c, k):
        return pltpu.make_async_remote_copy(
            src_ref=G.at[c, x, z], dst_ref=G.at[c, x, z],
            send_sem=gs.at[c], recv_sem=gr.at[c],
            device_id=z_peer(k), device_id_type=MESH,
        )

    def xg_send(c):
        return pltpu.make_async_remote_copy(
            src_ref=G.at[c, x], dst_ref=G.at[c, x],
            send_sem=xgs.at[c], recv_sem=xgr.at[c],
            device_id=peer_x, device_id_type=MESH,
        )

    def h_send(c, cross):
        return pltpu.make_async_remote_copy(
            src_ref=G.at[c, x, pl.ds(14, 2)], dst_ref=H.at[c, x],
            send_sem=hs.at[c, cross], recv_sem=hr.at[c, cross],
            device_id=(z * 2 + (xo if cross else x), dom + 1), device_id_type=MESH,
        )

    def all_bytes(c, sem):
        return pltpu.make_async_copy(RZ.at[c], RZ.at[c], sem.at[c])

    def advance(c):
        @pl.when(has_up)
        def _():
            for array in range(3):
                halo(0, array, c).wait_recv()

        @pl.when(has_down)
        def _():
            for array in range(3):
                halo(1, array, c).wait_recv()

        every = range(6)
        step(D, A, -4, 10, c, 4 * c, every)
        step(A, B, -3, 9, c, 0, every)
        step(B, A, -2, 8, c, 0, every)
        step(A, B, -1, 7, c, 0, range(1, 5))
        w6, w7, w8 = (coef * k for k in keep)
        for a in range(4):
            s = [B[r + 5, a + 1] for r in range(-1, 8)]
            prev, s = s[0], s[1:]
            weighted = [
                w8 * (s[0] - 0.5 * (prev + s[1])),
                w7 * (s[1] - 0.5 * (prev + s[3])),
                w8 * (s[2] - 0.5 * (s[1] + s[3])),
                w6 * (s[3] - 0.5 * (prev + s[7])),
                w8 * (s[4] - 0.5 * (s[3] + s[5])),
                w7 * (s[5] - 0.5 * (s[3] + s[7])),
                w8 * (s[6] - 0.5 * (s[5] + s[7])),
                coef * s[7],
            ]
            for r in range(8):
                W[c, a // 2, 2 * r + a % 2] = weighted[r]
        x_send(c).start()

    def pair_sum(c):
        x_send(c).wait_recv()
        for p in range(16):
            PZ[c, p] = W[c, x, p] + RX[c, p]
        if c == 0:

            @pl.when(z < Z - 1)
            def _():
                pl.semaphore_wait(open_sem, 1)

        for k in FAR_FIRST:
            z_send(c, k).start()

    def ring_sum(c):
        all_bytes(c, zr).wait()
        total = PZ[c, z]
        for k in range(15):
            total = total + RZ[c, k]
        G[c, x, z] = total
        for k in FAR_FIRST:
            g_send(c, k).start()

    def share(c):
        all_bytes(c, gr).wait()
        xg_send(c).start()

        @pl.when(has_down)
        def _():
            h_send(c, 0).start()
            h_send(c, 1).start()

    def nodal(c):
        xg_send(c).wait_recv()

        @pl.when(has_up)
        def _():
            h_send(c, 0).wait_recv()
            h_send(c, 1).wait_recv()

        m6, m7, m8 = keep
        for a in range(4):
            t = [G[c, a // 2, 2 * r + a % 2] for r in range(8)]
            prev = H[c, a // 2, a % 2]
            o7 = t[7]
            o3 = 0.5 * (prev + o7) + m6 * t[3]
            o1 = 0.5 * (prev + o3) + m7 * t[1]
            o5 = 0.5 * (o3 + o7) + m7 * t[5]
            o0 = 0.5 * (prev + o1) + m8 * t[0]
            o2 = 0.5 * (o1 + o3) + m8 * t[2]
            o4 = 0.5 * (o3 + o5) + m8 * t[4]
            o6 = 0.5 * (o5 + o7) + m8 * t[6]
            for r, o in enumerate((o0, o1, o2, o3, o4, o5, o6, o7)):
                out_ref[pl.ds((4 * c + a) * 8 + r, 8, stride=128), :] = o

    @pl.when(dom == 0)
    def _():
        H[...] = jnp.zeros((CHUNKS, 2, 2, 8, 128), jnp.float32)

    for stage, c in (
        (advance, 0), (advance, 1), (pair_sum, 0), (advance, 2), (pair_sum, 1), (advance, 3), (pair_sum, 2),
        (ring_sum, 0), (pair_sum, 3), (ring_sum, 1), (ring_sum, 2), (share, 0), (ring_sum, 3), (share, 1),
        (nodal, 0), (share, 2), (nodal, 1), (share, 3), (nodal, 2), (nodal, 3),
    ):
        stage(c)

    for c in range(CHUNKS):
        x_send(c).wait_send()
        all_bytes(c, zs).wait()
        all_bytes(c, gs).wait()
        xg_send(c).wait_send()

        @pl.when(has_down)
        def _():
            for array in range(3):
                halo(0, array, c).wait_send()
            h_send(c, 0).wait_send()
            h_send(c, 1).wait_send()

        @pl.when(has_up)
        def _():
            for array in range(3):
                halo(1, array, c).wait_send()


def on_device(density, diffusion, drift_speed, levels, coefficient):
    def tiles(block):
        return block.reshape(8, 128, 128).transpose(1, 0, 2).reshape(1024, 128)

    f32 = jnp.float32
    out = pl.pallas_call(
        kernel,
        out_shape=jax.ShapeDtypeStruct((1024, 128), f32),
        in_specs=[pl.BlockSpec(memory_space=pltpu.SMEM)] * 2 + [pl.BlockSpec(memory_space=pl.ANY)] * 3,
        out_specs=pl.BlockSpec(memory_space=pltpu.VMEM),
        scratch_shapes=[
            pltpu.VMEM((1024, 128), f32),
            pltpu.VMEM((1024, 128), f32),
            pltpu.VMEM((1024, 128), f32),
            pltpu.VMEM((17, 18, 8, 128), f32),
            pltpu.VMEM((15, 18, 8, 128), f32),
            pltpu.VMEM((15, 18, 8, 128), f32),
            pltpu.VMEM((17, 6, 8, 128), f32),
            pltpu.VMEM((17, 6, 8, 128), f32),
            pltpu.VMEM((CHUNKS, 2, 16, 8, 128), f32),
            pltpu.VMEM((CHUNKS, 16, 8, 128), f32),
            pltpu.VMEM((CHUNKS, 16, 8, 128), f32),
            pltpu.VMEM((CHUNKS, 15, 8, 128), f32),
            pltpu.VMEM((CHUNKS, 2, 16, 8, 128), f32),
            pltpu.VMEM((CHUNKS, 2, 2, 8, 128), f32),
            pltpu.SemaphoreType.DMA((3,)),
            pltpu.SemaphoreType.DMA((2, 3, CHUNKS)),
            pltpu.SemaphoreType.DMA((2, 3, CHUNKS)),
            pltpu.SemaphoreType.REGULAR,
            pltpu.SemaphoreType.REGULAR,
            pltpu.SemaphoreType.DMA((CHUNKS,)),
            pltpu.SemaphoreType.DMA((CHUNKS,)),
            pltpu.SemaphoreType.DMA((CHUNKS,)),
            pltpu.SemaphoreType.DMA((CHUNKS,)),
            pltpu.SemaphoreType.DMA((CHUNKS,)),
            pltpu.SemaphoreType.DMA((CHUNKS,)),
            pltpu.SemaphoreType.DMA((CHUNKS,)),
            pltpu.SemaphoreType.DMA((CHUNKS,)),
            pltpu.SemaphoreType.DMA((CHUNKS, 2)),
            pltpu.SemaphoreType.DMA((CHUNKS, 2)),
        ],
        compiler_params=pltpu.CompilerParams(collective_id=0, has_side_effects=True, vmem_limit_bytes=54500 * 1024),
        name="combine",
    )(levels, coefficient, tiles(density[0]), tiles(diffusion[0]), tiles(drift_speed[0]))
    return out.reshape(128, 8, 128).transpose(1, 0, 2).reshape(1, 8, 16384)


def solution(mesh):
    return jax.shard_map(
        on_device,
        mesh=mesh,
        in_specs=(
            P("grp", "dom", None),
            P("grp", "dom", None),
            P("grp", "dom", None),
            P("grp"),
            P("grp"),
        ),
        out_specs=P("grp", "dom", None),
        check_vma=False,
    )
```

```python
import jax
import jax.numpy as jnp
from jax import lax
from jax.experimental import pallas as pl
from jax.experimental.pallas import tpu as pltpu
from jax.sharding import PartitionSpec as P

MESH = pl.DeviceIdType.MESH
CHUNKS = 4
Z = 16
DOM = 32
EDGES = ((0, 6), (6, 10), (10, 14), (14, 18))
FAR_FIRST = (8, 7, 9, 6, 10, 5, 11, 4, 12, 3, 13, 2, 14, 1, 15)


def kernel(
    lev_ref, coef_ref, den_ref, dif_ref, dri_ref, out_ref,
    in_d, in_k, in_v, D, K, V, A, B, W, RX, PZ, RZ, G, H,
    load_sem, halo_send, halo_recv, chain_sem, open_sem, first_sem, late_sem, xs, xr, zs, zr, gs, gr, xgs, xgr, hs, hr,
):
    grp = lax.axis_index("grp")
    dom = lax.axis_index("dom")
    z = grp // 2
    x = grp % 2
    xo = 1 - x
    has_up = dom > 0
    has_down = dom < DOM - 1
    peer_x = (z * 2 + xo, dom)

    def z_peer(k):
        return (((z + k + Z) % Z) * 2 + x, dom)

    loads = [
        pltpu.make_async_copy(src, dst, load_sem.at[i])
        for i, (src, dst) in enumerate(((den_ref, in_d), (dif_ref, in_k), (dri_ref, in_v)))
    ]
    for load in loads:
        load.start()

    barrier = pltpu.get_barrier_semaphore()

    def greet(device):
        pl.semaphore_signal(barrier, inc=1, device_id=device, device_id_type=MESH)

    greet(peer_x)

    @pl.when(z > 0)
    def _():
        greet(z_peer(-1))

    @pl.when((z > 0) & (z < Z - 1))
    def _():
        greet(z_peer(1))

    @pl.when(has_up)
    def _():
        greet((grp, dom - 1))
        greet((z * 2 + xo, dom - 1))

    @pl.when(has_down)
    def _():
        greet((grp, dom + 1))
        greet((z * 2 + xo, dom + 1))

    sub = lax.broadcasted_iota(jnp.int32, (8, 128), 0)
    lane = lax.broadcasted_iota(jnp.int32, (8, 128), 1)
    zero = jnp.zeros((8, 128), jnp.float32)

    @pl.when(dom == 0)
    def _():
        D[0:5] = jnp.zeros((5, 18, 8, 128), jnp.float32)
        K[0:4] = jnp.zeros((4, 18, 8, 128), jnp.float32)
        V[0:4] = jnp.zeros((4, 18, 8, 128), jnp.float32)

    @pl.when(dom == DOM - 1)
    def _():
        D[13:17] = jnp.zeros((4, 18, 8, 128), jnp.float32)
        K[12:15] = jnp.zeros((3, 18, 8, 128), jnp.float32)
        V[12:15] = jnp.zeros((3, 18, 8, 128), jnp.float32)

    def halo(direction, array, c):
        lo, hi = EDGES[c]
        ref = (D, K, V)[array]
        if direction == 0:
            src, dst, n = (8, 0, 5) if array == 0 else (8, 0, 4)
            to = (grp, dom + 1)
        else:
            src, dst, n = (5, 13, 4) if array == 0 else (4, 12, 3)
            to = (grp, dom - 1)
        return pltpu.make_async_remote_copy(
            src_ref=ref.at[pl.ds(src, n), pl.ds(lo, hi - lo)],
            dst_ref=ref.at[pl.ds(dst, n), pl.ds(lo, hi - lo)],
            send_sem=halo_send.at[direction, array, c],
            recv_sem=halo_recv.at[direction, array, c],
            device_id=to,
            device_id_type=MESH,
        )

    def spread(c):
        for source, ref, first in ((in_d, D, 5), (in_k, K, 4), (in_v, V, 4)):
            for e in range(*EDGES[c]):
                for r in range(8):
                    a = (e - 1) % 16
                    tile = source[pl.ds(a * 8 + r, 8, stride=128), :]
                    if e == 0:
                        tile = jnp.where(sub == 0, zero, pltpu.roll(tile, 1, 0))
                    if e == 17:
                        tile = jnp.where(sub == 7, zero, pltpu.roll(tile, 7, 0))
                    ref[first + r, e] = tile

    def pass_token():
        @pl.when(z == 0)
        def _():
            pl.semaphore_signal(first_sem, inc=1, device_id=z_peer(1), device_id_type=MESH)

        @pl.when(z > 1)
        def _():
            pl.semaphore_wait(chain_sem, 1)

        @pl.when((z > 0) & (z < Z - 1))
        def _():
            pl.semaphore_signal(chain_sem, inc=1, device_id=z_peer(1), device_id_type=MESH)

        @pl.when(z == Z - 1)
        def _():
            for k in FAR_FIRST:
                if k != 1:
                    pl.semaphore_signal(open_sem, inc=1, device_id=z_peer(k), device_id_type=MESH)

    for load in loads:
        load.wait()
    for c in range(CHUNKS):
        spread(c)
        if c == 0:
            pl.semaphore_wait(
                barrier,
                1 + (z > 1).astype(jnp.int32) + (z < Z - 1).astype(jnp.int32)
                + 2 * has_up.astype(jnp.int32) + 2 * has_down.astype(jnp.int32),
            )

        @pl.when(has_down)
        def _():
            for array in range(3):
                halo(0, array, c).start()

        @pl.when(has_up)
        def _():
            for array in range(3):
                halo(1, array, c).start()

        if c == 0:
            pass_token()

    def most_begun():
        @pl.when(z < Z - 1)
        def _():
            pl.semaphore_wait(open_sem, 1)

        @pl.when(z == 1)
        def _():
            pl.semaphore_wait(first_sem, 1)
            pl.semaphore_signal(open_sem, inc=1, device_id=z_peer(-1), device_id_type=MESH)
            for k in range(1, Z - 1):
                pl.semaphore_signal(late_sem, inc=1, device_id=z_peer(k), device_id_type=MESH)

    def first_begun():
        @pl.when(z > 1)
        def _():
            pl.semaphore_wait(late_sem, 1)

    level = lev_ref[0]
    coef = coef_ref[0].astype(jnp.float32)
    keep = [
        jnp.minimum(jnp.maximum(level - (finest - 1), 0), 1).astype(jnp.float32)
        for finest in (6, 7, 8)
    ]

    def step(src, dst, first, last, c, offset, inner):
        for r in range(first, last + 1):
            mid = [src[r + 5, offset + j] for j in range(6)]
            from_left = [pltpu.roll(t, 1, 1) for t in mid]
            from_right = [pltpu.roll(t, 127, 1) for t in mid]
            for j in inner:
                left = from_left[j]
                right = from_right[j]
                if j > 0:
                    left = jnp.where(lane == 0, from_left[j - 1], left)
                if j < 5:
                    right = jnp.where(lane == 127, from_right[j + 1], right)
                below = src[r + 4, offset + j]
                above = src[r + 6, offset + j]
                dst[r + 5, j] = (
                    mid[j]
                    + K[r + 4, 4 * c + j] * (above + below + right + left - 4.0 * mid[j])
                    - 0.5 * V[r + 4, 4 * c + j] * (above - below)
                )

    def x_send(c):
        return pltpu.make_async_remote_copy(
            src_ref=W.at[c, xo], dst_ref=RX.at[c],
            send_sem=xs.at[c], recv_sem=xr.at[c],
            device_id=peer_x, device_id_type=MESH,
        )

    def z_send(c, k):
        return pltpu.make_async_remote_copy(
            src_ref=PZ.at[c, (z + k) % Z], dst_ref=RZ.at[c, k - 1],
            send_sem=zs.at[c], recv_sem=zr.at[c],
            device_id=z_peer(k), device_id_type=MESH,
        )

    def z_to_first(c):
        return pltpu.make_async_remote_copy(
            src_ref=PZ.at[c, 0], dst_ref=RZ.at[c, Z - 1 - z],
            send_sem=zs.at[c], recv_sem=zr.at[c],
            device_id=(x, dom), device_id_type=MESH,
        )

    def g_send(c, k):
        return pltpu.make_async_remote_copy(
            src_ref=G.at[c, x, z], dst_ref=G.at[c, x, z],
            send_sem=gs.at[c], recv_sem=gr.at[c],
            device_id=z_peer(k), device_id_type=MESH,
        )

    def xg_send(c):
        return pltpu.make_async_remote_copy(
            src_ref=G.at[c, x], dst_ref=G.at[c, x],
            send_sem=xgs.at[c], recv_sem=xgr.at[c],
            device_id=peer_x, device_id_type=MESH,
        )

    def h_send(c, cross):
        return pltpu.make_async_remote_copy(
            src_ref=G.at[c, x, pl.ds(14, 2)], dst_ref=H.at[c, x],
            send_sem=hs.at[c, cross], recv_sem=hr.at[c, cross],
            device_id=(z * 2 + (xo if cross else x), dom + 1), device_id_type=MESH,
        )

    def all_bytes(c, sem):
        return pltpu.make_async_copy(RZ.at[c], RZ.at[c], sem.at[c])

    def advance(c):
        @pl.when(has_up)
        def _():
            for array in range(3):
                halo(0, array, c).wait_recv()

        @pl.when(has_down)
        def _():
            for array in range(3):
                halo(1, array, c).wait_recv()

        every = range(6)
        step(D, A, -4, 10, c, 4 * c, every)
        step(A, B, -3, 9, c, 0, every)
        step(B, A, -2, 8, c, 0, every)
        step(A, B, -1, 7, c, 0, range(1, 5))
        w6, w7, w8 = (coef * k for k in keep)
        for a in range(4):
            s = [B[r + 5, a + 1] for r in range(-1, 8)]
            prev, s = s[0], s[1:]
            weighted = [
                w8 * (s[0] - 0.5 * (prev + s[1])),
                w7 * (s[1] - 0.5 * (prev + s[3])),
                w8 * (s[2] - 0.5 * (s[1] + s[3])),
                w6 * (s[3] - 0.5 * (prev + s[7])),
                w8 * (s[4] - 0.5 * (s[3] + s[5])),
                w7 * (s[5] - 0.5 * (s[3] + s[7])),
                w8 * (s[6] - 0.5 * (s[5] + s[7])),
                coef * s[7],
            ]
            for r in range(8):
                W[c, a // 2, 2 * r + a % 2] = weighted[r]
        x_send(c).start()

    def pair_sum(c):
        x_send(c).wait_recv()
        for p in range(16):
            PZ[c, p] = W[c, x, p] + RX[c, p]
        if c == 0:
            most_begun()
        if c == 1:
            first_begun()

            @pl.when(z > 0)
            def _():
                z_to_first(0).start()

        for k in FAR_FIRST:
            if c > 0:
                z_send(c, k).start()
            else:

                @pl.when((z + k) % Z != 0)
                def _():
                    z_send(c, k).start()

    def ring_sum(c):
        all_bytes(c, zr).wait()
        total = PZ[c, z]
        for k in range(15):
            total = total + RZ[c, k]
        G[c, x, z] = total
        for k in FAR_FIRST:
            g_send(c, k).start()

    def share(c):
        all_bytes(c, gr).wait()
        xg_send(c).start()

        @pl.when(has_down)
        def _():
            h_send(c, 0).start()
            h_send(c, 1).start()

    def nodal(c):
        xg_send(c).wait_recv()

        @pl.when(has_up)
        def _():
            h_send(c, 0).wait_recv()
            h_send(c, 1).wait_recv()

        m6, m7, m8 = keep
        for a in range(4):
            t = [G[c, a // 2, 2 * r + a % 2] for r in range(8)]
            prev = H[c, a // 2, a % 2]
            o7 = t[7]
            o3 = 0.5 * (prev + o7) + m6 * t[3]
            o1 = 0.5 * (prev + o3) + m7 * t[1]
            o5 = 0.5 * (o3 + o7) + m7 * t[5]
            o0 = 0.5 * (prev + o1) + m8 * t[0]
            o2 = 0.5 * (o1 + o3) + m8 * t[2]
            o4 = 0.5 * (o3 + o5) + m8 * t[4]
            o6 = 0.5 * (o5 + o7) + m8 * t[6]
            for r, o in enumerate((o0, o1, o2, o3, o4, o5, o6, o7)):
                out_ref[pl.ds((4 * c + a) * 8 + r, 8, stride=128), :] = o

    @pl.when(dom == 0)
    def _():
        H[...] = jnp.zeros((CHUNKS, 2, 2, 8, 128), jnp.float32)

    for stage, c in (
        (advance, 0), (advance, 1), (pair_sum, 0), (advance, 2), (pair_sum, 1), (advance, 3), (pair_sum, 2),
        (ring_sum, 0), (pair_sum, 3), (ring_sum, 1), (ring_sum, 2), (share, 0), (ring_sum, 3), (share, 1),
        (nodal, 0), (share, 2), (nodal, 1), (share, 3), (nodal, 2), (nodal, 3),
    ):
        stage(c)

    for c in range(CHUNKS):
        x_send(c).wait_send()
        all_bytes(c, zs).wait()
        all_bytes(c, gs).wait()
        xg_send(c).wait_send()

        @pl.when(has_down)
        def _():
            for array in range(3):
                halo(0, array, c).wait_send()
            h_send(c, 0).wait_send()
            h_send(c, 1).wait_send()

        @pl.when(has_up)
        def _():
            for array in range(3):
                halo(1, array, c).wait_send()


def on_device(density, diffusion, drift_speed, levels, coefficient):
    def tiles(block):
        return block.reshape(8, 128, 128).transpose(1, 0, 2).reshape(1024, 128)

    f32 = jnp.float32
    out = pl.pallas_call(
        kernel,
        out_shape=jax.ShapeDtypeStruct((1024, 128), f32),
        in_specs=[pl.BlockSpec(memory_space=pltpu.SMEM)] * 2 + [pl.BlockSpec(memory_space=pl.ANY)] * 3,
        out_specs=pl.BlockSpec(memory_space=pltpu.VMEM),
        scratch_shapes=[
            pltpu.VMEM((1024, 128), f32),
            pltpu.VMEM((1024, 128), f32),
            pltpu.VMEM((1024, 128), f32),
            pltpu.VMEM((17, 18, 8, 128), f32),
            pltpu.VMEM((15, 18, 8, 128), f32),
            pltpu.VMEM((15, 18, 8, 128), f32),
            pltpu.VMEM((17, 6, 8, 128), f32),
            pltpu.VMEM((17, 6, 8, 128), f32),
            pltpu.VMEM((CHUNKS, 2, 16, 8, 128), f32),
            pltpu.VMEM((CHUNKS, 16, 8, 128), f32),
            pltpu.VMEM((CHUNKS, 16, 8, 128), f32),
            pltpu.VMEM((CHUNKS, 15, 8, 128), f32),
            pltpu.VMEM((CHUNKS, 2, 16, 8, 128), f32),
            pltpu.VMEM((CHUNKS, 2, 2, 8, 128), f32),
            pltpu.SemaphoreType.DMA((3,)),
            pltpu.SemaphoreType.DMA((2, 3, CHUNKS)),
            pltpu.SemaphoreType.DMA((2, 3, CHUNKS)),
            pltpu.SemaphoreType.REGULAR,
            pltpu.SemaphoreType.REGULAR,
            pltpu.SemaphoreType.REGULAR,
            pltpu.SemaphoreType.REGULAR,
            pltpu.SemaphoreType.DMA((CHUNKS,)),
            pltpu.SemaphoreType.DMA((CHUNKS,)),
            pltpu.SemaphoreType.DMA((CHUNKS,)),
            pltpu.SemaphoreType.DMA((CHUNKS,)),
            pltpu.SemaphoreType.DMA((CHUNKS,)),
            pltpu.SemaphoreType.DMA((CHUNKS,)),
            pltpu.SemaphoreType.DMA((CHUNKS,)),
            pltpu.SemaphoreType.DMA((CHUNKS,)),
            pltpu.SemaphoreType.DMA((CHUNKS, 2)),
            pltpu.SemaphoreType.DMA((CHUNKS, 2)),
        ],
        compiler_params=pltpu.CompilerParams(collective_id=0, has_side_effects=True, vmem_limit_bytes=54500 * 1024),
        name="combine",
    )(levels, coefficient, tiles(density[0]), tiles(diffusion[0]), tiles(drift_speed[0]))
    return out.reshape(128, 8, 128).transpose(1, 0, 2).reshape(1, 8, 16384)


def solution(mesh):
    return jax.shard_map(
        on_device,
        mesh=mesh,
        in_specs=(
            P("grp", "dom", None),
            P("grp", "dom", None),
            P("grp", "dom", None),
            P("grp"),
            P("grp"),
        ),
        out_specs=P("grp", "dom", None),
        check_vma=False,
    )
```

```python
import jax
import jax.numpy as jnp
from jax import lax
from jax.experimental import pallas as pl
from jax.experimental.pallas import tpu as pltpu
from jax.sharding import PartitionSpec as P

MESH = pl.DeviceIdType.MESH
CHUNKS = 4
Z = 16
DOM = 32
EDGES = ((0, 6), (6, 10), (10, 14), (14, 18))
FAR_FIRST = (8, 7, 9, 6, 10, 5, 11, 4, 12, 3, 13, 2, 14, 1, 15)


def kernel(
    lev_ref, coef_ref, den_ref, dif_ref, dri_ref, out_ref,
    in_d, in_k, in_v, D, K, V, A, B, W, RX, PZ, RZ, G, H,
    load_sem, halo_send, halo_recv, chain_sem, open_sem, first_sem, late_sem, xs, xr, zs, zr, gs, gr, xgs, xgr, hs, hr,
):
    grp = lax.axis_index("grp")
    dom = lax.axis_index("dom")
    z = grp // 2
    x = grp % 2
    xo = 1 - x
    has_up = dom > 0
    has_down = dom < DOM - 1
    peer_x = (z * 2 + xo, dom)

    def z_peer(k):
        return (((z + k + Z) % Z) * 2 + x, dom)

    loads = [
        pltpu.make_async_copy(src, dst, load_sem.at[i])
        for i, (src, dst) in enumerate(((den_ref, in_d), (dif_ref, in_k), (dri_ref, in_v)))
    ]
    for load in loads:
        load.start()

    barrier = pltpu.get_barrier_semaphore()

    def greet(device):
        pl.semaphore_signal(barrier, inc=1, device_id=device, device_id_type=MESH)

    greet(peer_x)

    @pl.when(z > 0)
    def _():
        greet(z_peer(-1))

    @pl.when((z > 0) & (z < Z - 1))
    def _():
        greet(z_peer(1))

    @pl.when(has_up)
    def _():
        greet((grp, dom - 1))
        greet((z * 2 + xo, dom - 1))

    @pl.when(has_down)
    def _():
        greet((grp, dom + 1))
        greet((z * 2 + xo, dom + 1))

    sub = lax.broadcasted_iota(jnp.int32, (8, 128), 0)
    lane = lax.broadcasted_iota(jnp.int32, (8, 128), 1)
    zero = jnp.zeros((8, 128), jnp.float32)

    @pl.when(dom == 0)
    def _():
        D[0:5] = jnp.zeros((5, 18, 8, 128), jnp.float32)
        K[0:4] = jnp.zeros((4, 18, 8, 128), jnp.float32)
        V[0:4] = jnp.zeros((4, 18, 8, 128), jnp.float32)

    @pl.when(dom == DOM - 1)
    def _():
        D[13:17] = jnp.zeros((4, 18, 8, 128), jnp.float32)
        K[12:15] = jnp.zeros((3, 18, 8, 128), jnp.float32)
        V[12:15] = jnp.zeros((3, 18, 8, 128), jnp.float32)

    def halo(direction, array, c):
        lo, hi = EDGES[c]
        hi = min(hi, 17)
        ref = (D, K, V)[array]
        if direction == 0:
            src, dst, n = (8, 0, 5) if array == 0 else (8, 0, 4)
            to = (grp, dom + 1)
        else:
            src, dst, n = (5, 13, 4) if array == 0 else (4, 12, 3)
            to = (grp, dom - 1)
        return pltpu.make_async_remote_copy(
            src_ref=ref.at[pl.ds(src, n), pl.ds(lo, hi - lo)],
            dst_ref=ref.at[pl.ds(dst, n), pl.ds(lo, hi - lo)],
            send_sem=halo_send.at[direction, array, c],
            recv_sem=halo_recv.at[direction, array, c],
            device_id=to,
            device_id_type=MESH,
        )

    def spread(c):
        for source, ref, first in ((in_d, D, 5), (in_k, K, 4), (in_v, V, 4)):
            for e in range(*EDGES[c]):
                for r in range(8):
                    a = (e - 1) % 16
                    tile = source[pl.ds(a * 8 + r, 8, stride=128), :]
                    if e == 0:
                        tile = jnp.where(sub == 0, zero, pltpu.roll(tile, 1, 0))
                    if e == 17:
                        tile = jnp.where(sub == 7, zero, pltpu.roll(tile, 7, 0))
                    ref[first + r, e] = tile

    def pass_token():
        @pl.when(z == 0)
        def _():
            pl.semaphore_signal(first_sem, inc=1, device_id=z_peer(1), device_id_type=MESH)

        @pl.when(z > 1)
        def _():
            pl.semaphore_wait(chain_sem, 1)

        @pl.when((z > 0) & (z < Z - 1))
        def _():
            pl.semaphore_signal(chain_sem, inc=1, device_id=z_peer(1), device_id_type=MESH)

        @pl.when(z == Z - 1)
        def _():
            for k in FAR_FIRST:
                if k != 1:
                    pl.semaphore_signal(open_sem, inc=1, device_id=z_peer(k), device_id_type=MESH)

    for load in loads:
        load.wait()
    for c in range(CHUNKS):
        spread(c)
        if c == 0:
            pl.semaphore_wait(
                barrier,
                1 + (z > 1).astype(jnp.int32) + (z < Z - 1).astype(jnp.int32)
                + 2 * has_up.astype(jnp.int32) + 2 * has_down.astype(jnp.int32),
            )

        @pl.when(has_down)
        def _():
            for array in range(3):
                halo(0, array, c).start()

        @pl.when(has_up)
        def _():
            for array in range(3):
                halo(1, array, c).start()

        if c == 0:
            pass_token()

    def most_begun():
        @pl.when(z < Z - 1)
        def _():
            pl.semaphore_wait(open_sem, 1)

        @pl.when(z == 1)
        def _():
            pl.semaphore_wait(first_sem, 1)
            pl.semaphore_signal(open_sem, inc=1, device_id=z_peer(-1), device_id_type=MESH)
            for k in range(1, Z - 1):
                pl.semaphore_signal(late_sem, inc=1, device_id=z_peer(k), device_id_type=MESH)

    def first_begun():
        @pl.when(z > 1)
        def _():
            pl.semaphore_wait(late_sem, 1)

    level = lev_ref[0]
    coef = coef_ref[0].astype(jnp.float32)
    keep = [
        jnp.minimum(jnp.maximum(level - (finest - 1), 0), 1).astype(jnp.float32)
        for finest in (6, 7, 8)
    ]

    def step(src, dst, first, last, c, offset, inner):
        for r in range(first, last + 1):
            mid = [src[r + 5, offset + j] for j in range(6)]
            from_left = [pltpu.roll(t, 1, 1) for t in mid]
            from_right = [pltpu.roll(t, 127, 1) for t in mid]
            for j in inner:
                left = from_left[j]
                right = from_right[j]
                if j > 0:
                    left = jnp.where(lane == 0, from_left[j - 1], left)
                if j < 5:
                    right = jnp.where(lane == 127, from_right[j + 1], right)
                below = src[r + 4, offset + j]
                above = src[r + 6, offset + j]
                dst[r + 5, j] = (
                    mid[j]
                    + K[r + 4, 4 * c + j] * (above + below + right + left - 4.0 * mid[j])
                    - 0.5 * V[r + 4, 4 * c + j] * (above - below)
                )

    def x_send(c):
        return pltpu.make_async_remote_copy(
            src_ref=W.at[c, xo], dst_ref=RX.at[c],
            send_sem=xs.at[c], recv_sem=xr.at[c],
            device_id=peer_x, device_id_type=MESH,
        )

    def z_send(c, k):
        return pltpu.make_async_remote_copy(
            src_ref=PZ.at[c, (z + k) % Z], dst_ref=RZ.at[c, k - 1],
            send_sem=zs.at[c], recv_sem=zr.at[c],
            device_id=z_peer(k), device_id_type=MESH,
        )

    def z_to_first(c):
        return pltpu.make_async_remote_copy(
            src_ref=PZ.at[c, 0], dst_ref=RZ.at[c, Z - 1 - z],
            send_sem=zs.at[c], recv_sem=zr.at[c],
            device_id=(x, dom), device_id_type=MESH,
        )

    def g_send(c, k):
        return pltpu.make_async_remote_copy(
            src_ref=G.at[c, x, z], dst_ref=G.at[c, x, z],
            send_sem=gs.at[c], recv_sem=gr.at[c],
            device_id=z_peer(k), device_id_type=MESH,
        )

    def xg_send(c):
        return pltpu.make_async_remote_copy(
            src_ref=G.at[c, x], dst_ref=G.at[c, x],
            send_sem=xgs.at[c], recv_sem=xgr.at[c],
            device_id=peer_x, device_id_type=MESH,
        )

    def h_send(c, cross):
        return pltpu.make_async_remote_copy(
            src_ref=G.at[c, x, pl.ds(14, 2)], dst_ref=H.at[c, x],
            send_sem=hs.at[c, cross], recv_sem=hr.at[c, cross],
            device_id=(z * 2 + (xo if cross else x), dom + 1), device_id_type=MESH,
        )

    def all_bytes(c, sem):
        return pltpu.make_async_copy(RZ.at[c], RZ.at[c], sem.at[c])

    def advance(c):
        @pl.when(has_up)
        def _():
            for array in range(3):
                halo(0, array, c).wait_recv()

        @pl.when(has_down)
        def _():
            for array in range(3):
                halo(1, array, c).wait_recv()

        if c == CHUNKS - 1:
            for ref, rows in ((D, (0, 5, 13, 17)), (K, (0, 4, 12, 15)), (V, (0, 4, 12, 15))):
                for r in (*range(rows[0], rows[1]), *range(rows[2], rows[3])):
                    ref[r, 17] = jnp.where(sub == 7, zero, pltpu.roll(ref[r, 1], 7, 0))
        every = range(6)
        step(D, A, -4, 10, c, 4 * c, every)
        step(A, B, -3, 9, c, 0, every)
        step(B, A, -2, 8, c, 0, every)
        step(A, B, -1, 7, c, 0, range(1, 5))
        w6, w7, w8 = (coef * k for k in keep)
        for a in range(4):
            s = [B[r + 5, a + 1] for r in range(-1, 8)]
            prev, s = s[0], s[1:]
            weighted = [
                w8 * (s[0] - 0.5 * (prev + s[1])),
                w7 * (s[1] - 0.5 * (prev + s[3])),
                w8 * (s[2] - 0.5 * (s[1] + s[3])),
                w6 * (s[3] - 0.5 * (prev + s[7])),
                w8 * (s[4] - 0.5 * (s[3] + s[5])),
                w7 * (s[5] - 0.5 * (s[3] + s[7])),
                w8 * (s[6] - 0.5 * (s[5] + s[7])),
                coef * s[7],
            ]
            for r in range(8):
                W[c, a // 2, 2 * r + a % 2] = weighted[r]
        x_send(c).start()

    def pair_sum(c):
        x_send(c).wait_recv()
        for p in range(16):
            PZ[c, p] = W[c, x, p] + RX[c, p]
        if c == 0:
            most_begun()
        if c == 1:
            first_begun()

            @pl.when(z > 0)
            def _():
                z_to_first(0).start()

        for k in FAR_FIRST:
            if c > 0:
                z_send(c, k).start()
            else:

                @pl.when((z + k) % Z != 0)
                def _():
                    z_send(c, k).start()

    def ring_sum(c):
        all_bytes(c, zr).wait()
        total = PZ[c, z]
        for k in range(15):
            total = total + RZ[c, k]
        G[c, x, z] = total
        for k in FAR_FIRST:
            g_send(c, k).start()

    def share(c):
        all_bytes(c, gr).wait()
        xg_send(c).start()

        @pl.when(has_down)
        def _():
            h_send(c, 0).start()
            h_send(c, 1).start()

    def nodal(c):
        xg_send(c).wait_recv()

        @pl.when(has_up)
        def _():
            h_send(c, 0).wait_recv()
            h_send(c, 1).wait_recv()

        m6, m7, m8 = keep
        for a in range(4):
            t = [G[c, a // 2, 2 * r + a % 2] for r in range(8)]
            prev = H[c, a // 2, a % 2]
            o7 = t[7]
            o3 = 0.5 * (prev + o7) + m6 * t[3]
            o1 = 0.5 * (prev + o3) + m7 * t[1]
            o5 = 0.5 * (o3 + o7) + m7 * t[5]
            o0 = 0.5 * (prev + o1) + m8 * t[0]
            o2 = 0.5 * (o1 + o3) + m8 * t[2]
            o4 = 0.5 * (o3 + o5) + m8 * t[4]
            o6 = 0.5 * (o5 + o7) + m8 * t[6]
            for r, o in enumerate((o0, o1, o2, o3, o4, o5, o6, o7)):
                out_ref[pl.ds((4 * c + a) * 8 + r, 8, stride=128), :] = o

    @pl.when(dom == 0)
    def _():
        H[...] = jnp.zeros((CHUNKS, 2, 2, 8, 128), jnp.float32)

    for stage, c in (
        (advance, 0), (advance, 1), (pair_sum, 0), (advance, 2), (pair_sum, 1), (advance, 3), (pair_sum, 2),
        (ring_sum, 0), (pair_sum, 3), (ring_sum, 1), (ring_sum, 2), (share, 0), (ring_sum, 3), (share, 1),
        (nodal, 0), (share, 2), (nodal, 1), (share, 3), (nodal, 2), (nodal, 3),
    ):
        stage(c)

    for c in range(CHUNKS):
        x_send(c).wait_send()
        all_bytes(c, zs).wait()
        all_bytes(c, gs).wait()
        xg_send(c).wait_send()

        @pl.when(has_down)
        def _():
            for array in range(3):
                halo(0, array, c).wait_send()
            h_send(c, 0).wait_send()
            h_send(c, 1).wait_send()

        @pl.when(has_up)
        def _():
            for array in range(3):
                halo(1, array, c).wait_send()


def on_device(density, diffusion, drift_speed, levels, coefficient):
    def tiles(block):
        return block.reshape(8, 128, 128).transpose(1, 0, 2).reshape(1024, 128)

    f32 = jnp.float32
    out = pl.pallas_call(
        kernel,
        out_shape=jax.ShapeDtypeStruct((1024, 128), f32),
        in_specs=[pl.BlockSpec(memory_space=pltpu.SMEM)] * 2 + [pl.BlockSpec(memory_space=pl.ANY)] * 3,
        out_specs=pl.BlockSpec(memory_space=pltpu.VMEM),
        scratch_shapes=[
            pltpu.VMEM((1024, 128), f32),
            pltpu.VMEM((1024, 128), f32),
            pltpu.VMEM((1024, 128), f32),
            pltpu.VMEM((17, 18, 8, 128), f32),
            pltpu.VMEM((15, 18, 8, 128), f32),
            pltpu.VMEM((15, 18, 8, 128), f32),
            pltpu.VMEM((17, 6, 8, 128), f32),
            pltpu.VMEM((17, 6, 8, 128), f32),
            pltpu.VMEM((CHUNKS, 2, 16, 8, 128), f32),
            pltpu.VMEM((CHUNKS, 16, 8, 128), f32),
            pltpu.VMEM((CHUNKS, 16, 8, 128), f32),
            pltpu.VMEM((CHUNKS, 15, 8, 128), f32),
            pltpu.VMEM((CHUNKS, 2, 16, 8, 128), f32),
            pltpu.VMEM((CHUNKS, 2, 2, 8, 128), f32),
            pltpu.SemaphoreType.DMA((3,)),
            pltpu.SemaphoreType.DMA((2, 3, CHUNKS)),
            pltpu.SemaphoreType.DMA((2, 3, CHUNKS)),
            pltpu.SemaphoreType.REGULAR,
            pltpu.SemaphoreType.REGULAR,
            pltpu.SemaphoreType.REGULAR,
            pltpu.SemaphoreType.REGULAR,
            pltpu.SemaphoreType.DMA((CHUNKS,)),
            pltpu.SemaphoreType.DMA((CHUNKS,)),
            pltpu.SemaphoreType.DMA((CHUNKS,)),
            pltpu.SemaphoreType.DMA((CHUNKS,)),
            pltpu.SemaphoreType.DMA((CHUNKS,)),
            pltpu.SemaphoreType.DMA((CHUNKS,)),
            pltpu.SemaphoreType.DMA((CHUNKS,)),
            pltpu.SemaphoreType.DMA((CHUNKS,)),
            pltpu.SemaphoreType.DMA((CHUNKS, 2)),
            pltpu.SemaphoreType.DMA((CHUNKS, 2)),
        ],
        compiler_params=pltpu.CompilerParams(collective_id=0, has_side_effects=True, vmem_limit_bytes=54500 * 1024),
        name="combine",
    )(levels, coefficient, tiles(density[0]), tiles(diffusion[0]), tiles(drift_speed[0]))
    return out.reshape(128, 8, 128).transpose(1, 0, 2).reshape(1, 8, 16384)


def solution(mesh):
    return jax.shard_map(
        on_device,
        mesh=mesh,
        in_specs=(
            P("grp", "dom", None),
            P("grp", "dom", None),
            P("grp", "dom", None),
            P("grp"),
            P("grp"),
        ),
        out_specs=P("grp", "dom", None),
        check_vma=False,
    )
```
